256 devices in a mesh: op: 16 (over y, z_hi), right: 16 (over z_lo, x, core).
Axes of the slice: x: 4, y: 4, z: 8 (z_hi: 4, z_lo: 2; z = z_hi * 2 + z_lo), core: 2. Of those that a mesh axis runs over, the one named last changes fastest.
Arguments:
- psi: float32 [768, 16384], P('op', 'right'), may hold values from -6 to 6
- left_env: float32 [32, 768, 768], P('op', 'right'), may hold values from -0.078125 to 0.078125
- right_env: float32 [32, 16384, 1024], P('op', 'right'), may hold values from -0.1875 to 0.1875
- sector_lengths: int32 [4], replicated, may hold values from 128 to 384, as said below
- op_map: int32 [32, 4], replicated, may hold values from 0 to 3
Outputs:
- h_psi: float32 [768, 16384], P('op', 'right')
The draws below stay inside these ranges and needn't reach their ends.
Inputs may be any that keep to these rules, and one draw needn't show every extreme that they name: `sector_lengths`: one sector, at a position that varies between draws, holds 384 states; every other sector holds 128.
All inputs are finite; a program needn't handle non-finite values.
Results may differ from the reference program's by a relative error of at most 0.0003.
Values sent between devices are 32-bit elements; how exact they have to be, the bound alone decides.
A program may use at most 64 MiB of HBM per device.

```python
import jax
import jax.numpy as jnp
from jax import lax

A = 768
B_DEV = 1024
SECTORS = 4
PANEL = 128
W = 32
B = 16384
N_RIGHT = 16


def draw_sector_lengths(key, part):
    chosen = jax.random.randint(jax.random.fold_in(key, 7), (), 0, SECTORS).astype(jnp.int32)
    places = jnp.arange(SECTORS, dtype=jnp.int32)
    largest = A - (SECTORS - 1) * PANEL
    return jnp.where(places == chosen, largest, PANEL).astype(jnp.int32)


def plant(entries, own_key, low, top_value):
    longest = entries.shape.index(max(entries.shape))
    spots = []
    for shift in (0, 1):
        where = [jax.random.randint(jax.random.fold_in(own_key, axis), (), 0, length) for axis, length in enumerate(entries.shape)]
        where[longest] = (where[longest] + shift) % entries.shape[longest]
        spots.append(tuple(where))
    return entries.at[spots[0]].set(low).at[spots[1]].set(top_value)


def level_of(rng, extent, shards, smallest, high):
    def one(position, blocks):
        draws = jax.random.uniform(jax.random.fold_in(jax.random.fold_in(rng, 6), position), (blocks,), jnp.float32, smallest / len(shards), high / len(shards))
        return jnp.repeat(jnp.exp(draws), extent[position] // blocks).reshape((-1,) + (1,) * (len(extent) - position - 1))

    level = one(*shards[0])
    for cut in shards[1:]:
        level = level * one(*cut)
    return level


def bell_draw(stream_key, shape, width, bound, cuts=(), kind=jnp.bfloat16):
    entries = width * jax.random.normal(stream_key, shape, jnp.float32)
    if cuts:
        entries = entries * level_of(stream_key, shape, cuts, -0.22, 0.18)
    return jnp.clip(entries, -bound, bound).astype(kind)


def setup_inputs(seed: int = 0) -> dict:
    seeds = jax.random.split(jax.random.key(seed), 6)
    psi = bell_draw(seeds[0], (A, B), 1.0, 6.0, ((0, 16), (1, 16)), jnp.float32)
    left_env = bell_draw(seeds[1], (W, A, A), (A * W // SECTORS) ** -0.5, 0.078125, ((0, 16), (1, 16)), jnp.float32)
    right_env = bell_draw(seeds[2], (W, B, B_DEV), B_DEV ** -0.5, 0.1875, ((0, 16), (1, 16)), jnp.float32)
    sector_lengths = draw_sector_lengths(jax.random.fold_in(seeds[5], 71), 0)
    op_map = plant(jax.random.randint(seeds[4], (W, SECTORS), 0, SECTORS), jax.random.fold_in(seeds[4], 1), 0, SECTORS - 1).astype(jnp.int32)
    return dict(psi=psi, left_env=left_env, right_env=right_env, sector_lengths=sector_lengths, op_map=op_map)


def sector_of(sector_lengths):
    ends = jnp.cumsum(sector_lengths).astype(jnp.int32)
    places = jnp.arange(A, dtype=jnp.int32)
    return jnp.sum((places[:, None] >= ends[None, :]).astype(jnp.int32), axis=1).astype(jnp.int32)


def reference(psi, left_env, right_env, sector_lengths, op_map):
    sector = sector_of(sector_lengths)
    blocks = psi.reshape(A, N_RIGHT, B_DEV)

    def term(total, index):
        targets = op_map[index][sector]
        keep = (sector[:, None] == targets[None, :]).astype(jnp.float32)
        masked = left_env[index] * keep
        envs = right_env[index].reshape(N_RIGHT, B_DEV, B_DEV)
        inner = jnp.einsum("ajc,jbc->ajb", blocks, envs, precision=lax.Precision.HIGHEST).reshape(A, B)
        return total + jnp.dot(masked, inner, precision=lax.Precision.HIGHEST, preferred_element_type=jnp.float32), None

    total, unused = lax.scan(term, jnp.zeros((A, B), jnp.float32), jnp.arange(W, dtype=jnp.int32))
    return total
```

```python
import jax
import jax.numpy as jnp
from jax import lax
from jax.experimental import pallas as pl
from jax.experimental.pallas import tpu as pltpu
from jax.sharding import PartitionSpec as P

MESH = pl.DeviceIdType.MESH
BF = jnp.bfloat16
F32 = jnp.float32
I32 = jnp.int32

R = 48
HALF = R // 2
STATES = 768
BLOCK = 1024
TILE = 256
TILES = BLOCK // TILE
GROUP = 4 * R
UNITS = 4 * TILES
LAG_FAR = 2
LAG_NEAR = 4
ROWS_NT = (((1,), (1,)), ((), ()))
ROWS_NN = (((1,), (0,)), ((), ()))


def mod4(v):
    return lax.rem(v, 4)


def dot(a, b, dims):
    return lax.dot_general(a, b, dims, preferred_element_type=F32)


def halves(v):
    hi = v.astype(BF)
    return hi, (v - hi.astype(F32)).astype(BF)


def step_of(k):
    return mod4(2 + k + lax.div(k * (k - 1), 2))


def kernel(
    psi, left, renv, lengths, op_map, out,
    pg, lg, raw, rh, rl, p2, ih, il, m2, q, far, near, zfar, znear,
    local_sem, prs, pzs, pys, lrs, lls, lxs, lcs, fs, fr, ns, nr, zfs, zfr, zns, znr,
):
    op, right = lax.axis_index("op"), lax.axis_index("right")
    y, h = lax.div(op, 4), mod4(op)
    l, x, c = lax.div(right, 8), mod4(lax.div(right, 2)), lax.rem(right, 2)
    yp, ym, yf = mod4(y + 1), mod4(y + 3), mod4(y + 2)
    hp, hm, hf = mod4(h + 1), mod4(h + 3), mod4(h + 2)
    xp, xm, xf = mod4(x + 1), mod4(x + 3), mod4(x + 2)
    lo = 1 - l

    def op_at(a, b):
        return a * 4 + b

    def right_at(a, b, d):
        return a * 8 + b * 2 + d

    to_yp, to_ym = (op_at(yp, h), right), (op_at(ym, h), right)
    to_hp, to_hm = (op_at(y, hp), right), (op_at(y, hm), right)
    to_xp, to_xm = (op, right_at(l, xp, c)), (op, right_at(l, xm, c))
    to_l, to_c = (op, right_at(lo, x, c)), (op, right_at(l, x, 1 - c))

    barrier = pltpu.get_barrier_semaphore()
    partners = (to_yp, to_ym, to_hp, to_hm, to_xp, to_xm, to_l, to_c)
    for device in partners:
        pl.semaphore_signal(barrier, inc=1, device_id=device, device_id_type=MESH)

    load_env = pltpu.make_async_copy(renv, raw, local_sem.at[0])
    load_psi = pltpu.make_async_copy(psi, pg.at[op], local_sem.at[1])
    load_left = pltpu.make_async_copy(left, lg.at[right], local_sem.at[2])
    load_psi.start()
    load_env.start()
    load_left.start()
    pl.semaphore_wait(barrier, len(partners))

    def send(src, dst, ssem, rsem, device):
        copy = pltpu.make_async_remote_copy(
            src_ref=src, dst_ref=dst, send_sem=ssem, recv_sem=rsem, device_id=device, device_id_type=MESH
        )
        copy.start()

    def arrived(dst, ssem, rsem, device):
        pltpu.make_async_remote_copy(
            src_ref=dst, dst_ref=dst, send_sem=ssem, recv_sem=rsem, device_id=device, device_id_type=MESH
        ).wait_recv()

    def piece(o, half):
        return pg.at[o, pl.ds(half * HALF, HALF)]

    counts = {"z": 0, "y": 0, "l": 0, "x": 0, "c": 0}
    psi_sems, left_sems = {"z": pzs, "y": pys}, {"l": lls, "x": lxs, "c": lcs}

    def psi_send(axis, o, half, device, src=None):
        sem = psi_sems[axis].at[counts[axis]]
        counts[axis] += 1
        dst = piece(o, half)
        send(dst if src is None else src.at[pl.ds(half * HALF, HALF)], dst, sem, prs.at[o, half], device)

    def psi_arrived(o, half):
        arrived(piece(o, half), pzs.at[0], prs.at[o, half], to_yp)

    def left_send(axis, r, w, device, src=None):
        sem = left_sems[axis].at[counts[axis]]
        counts[axis] += 1
        dst = lg.at[r, w]
        send(dst if src is None else src.at[w], dst, sem, lrs.at[r, w], device)

    def left_arrived(r, w):
        arrived(lg.at[r, w], lls.at[0], lrs.at[r, w], to_xp)

    psi_send("z", op, 0, to_hp, psi)
    psi_send("z", op, 1, to_hm, psi)
    psi_send("y", op, 0, to_yp, psi)
    psi_send("y", op, 1, to_ym, psi)
    psi_send("z", op, 1, to_hp, psi)
    psi_send("z", op, 0, to_hm, psi)
    psi_send("y", op, 1, to_yp, psi)
    psi_send("y", op, 0, to_ym, psi)
    for w in (0, 1):
        left_send("x", right, w, to_xp, left)
        left_send("x", right, 1 - w, to_xm, left)
    for w in (0, 1):
        left_send("c", right, w, to_c, left)

    def both_ways(o, half):
        psi_send("y", o, half, to_yp)
        psi_send("y", o, half, to_ym)

    def from_below(o_h):
        psi_arrived(op_at(ym, o_h), 0)
        psi_send("y", op_at(ym, o_h), 0, to_yp)

    def from_above(o_h):
        psi_arrived(op_at(yp, o_h), 1)
        psi_send("y", op_at(yp, o_h), 1, to_ym)

    def rest_of(o_h):
        psi_arrived(op_at(ym, o_h), 1)
        psi_arrived(op_at(yp, o_h), 0)
        psi_arrived(op_at(yf, o_h), 0)
        psi_arrived(op_at(yf, o_h), 1)

    def to_group(i, o_h):
        for a in range(4):
            hi, low = halves(pg[op_at(a, o_h)])
            p2[i, a * R:(a + 1) * R] = hi
            p2[i, GROUP + a * R:GROUP + (a + 1) * R] = low

    def left_on(r, w):
        left_arrived(r, w)
        left_send("c", r, w, to_c)

    def inner_tile(i, o_h, w, t):
        rows = pl.ds(pl.multiple_of(w * BLOCK + t * TILE, TILE), TILE)
        both = dot(p2[i], rh[rows, :], ROWS_NT)
        cross = dot(p2[i, :GROUP], rl[rows, :], ROWS_NT)
        hi, low = halves(both[:GROUP] + both[GROUP:] + cross)
        for a in range(4):
            at = pl.ds(pl.multiple_of(w * STATES + op_at(a, o_h) * R, 16), R)
            ih[t, at, :] = hi[a * R:(a + 1) * R]
            il[t, at, :] = low[a * R:(a + 1) * R]

    load_env.wait()

    def split_env(s, carry):
        rows = pl.ds(pl.multiple_of(s * 32, 32), 32)
        hi, low = halves(raw[rows, :])
        rh[rows, :] = hi
        rl[rows, :] = low
        return carry

    lax.fori_loop(0, 2 * BLOCK // 32, split_env, 0)
    load_psi.wait()

    from_below(h)
    from_above(h)
    psi_arrived(op_at(y, hm), 0)
    psi_send("z", op_at(y, hm), 0, to_hp)
    both_ways(op_at(y, hm), 0)
    psi_arrived(op_at(y, hp), 1)
    psi_send("z", op_at(y, hp), 1, to_hm)
    both_ways(op_at(y, hp), 1)
    left_send("l", right, 0, to_l, left)
    left_send("l", right, 1, to_l, left)
    left_arrived(right_at(l, xm, c), 0)
    left_send("x", right_at(l, xm, c), 0, to_xp)
    left_send("c", right_at(l, xm, c), 0, to_c)
    left_arrived(right_at(l, xp, c), 1)
    left_send("x", right_at(l, xp, c), 1, to_xm)
    left_send("c", right_at(l, xp, c), 1, to_c)
    rest_of(h)
    to_group(0, h)

    def second_halves():
        psi_arrived(op_at(y, hp), 0)
        both_ways(op_at(y, hp), 0)
        psi_arrived(op_at(y, hm), 1)
        both_ways(op_at(y, hm), 1)

    def ready(i, o_h):
        rest_of(o_h)
        to_group(i, o_h)

    def farthest(half):
        psi_arrived(op_at(y, hf), half)
        both_ways(op_at(y, hf), half)

    def left_across(w):
        r = right_at(lo, x, c)
        left_arrived(r, w)
        left_send("x", r, w, to_xp)
        left_send("x", r, w, to_xm)
        left_send("c", r, w, to_c)

    def left_turn():
        r = right_at(lo, xm, c)
        left_arrived(r, 0)
        left_send("x", r, 0, to_xp)
        left_send("c", r, 0, to_c)
        r = right_at(lo, xp, c)
        left_arrived(r, 1)
        left_send("x", r, 1, to_xm)
        left_send("c", r, 1, to_c)

    def left_pair(a, b, second):
        left_on(right_at(a, b[0], c), second[0])
        left_on(right_at(a, b[1], c), second[1])

    events = {
        1: [(left_pair, l, (xm, xp), (1, 0))],
        2: [(second_halves,)],
        3: [(from_above, hp), (from_below, hp)],
        4: [(left_pair, l, (xf, xf), (0, 1))],
        5: [(left_across, 0)],
        6: [(from_below, hm)],
        7: [(left_across, 1)],
        8: [(ready, 1, hp)],
        9: [(farthest, 0)],
        10: [(farthest, 1)],
        11: [(from_above, hm)],
        13: [(left_turn,)],
        15: [(left_pair, lo, (xm, xp), (1, 0))],
        16: [(ready, 2, hm)],
        18: [(from_below, hf)],
        19: [(from_above, hf)],
        21: [(left_pair, lo, (xf, xf), (0, 1))],
    }

    def gather_step(e, carry):
        for at, calls in events.items():
            @pl.when(e == at)
            def _(calls=calls):
                for call, *rest in calls:
                    call(*rest)

        i = lax.div(e, 8)
        o_h = mod4(h + i + lax.div(i, 2))
        inner_tile(i, o_h, lax.rem(lax.div(e, 4), 2), mod4(e))
        return carry

    lax.fori_loop(0, 24, gather_step, 0)

    load_left.wait()
    for a in range(2):
        for b in range(4):
            for w in range(2):
                left_arrived(right_at(a, b, 1 - c), w)

    ends = []
    total = 0
    for k in range(4):
        total = total + lengths[k]
        ends.append(total)

    def sector_of(place):
        s = jnp.zeros(place.shape, I32)
        for end in ends:
            s = s + (place >= end).astype(I32)
        return s

    column_sector = sector_of(lax.broadcasted_iota(I32, (R, STATES), 1))
    targets = []
    for w in range(2):
        target = jnp.full((R, STATES), -1, I32)
        for k in range(4):
            target = jnp.where(column_sector == k, op_map[k, 2 * op + w], target)
        targets.append(target)

    def mask_rows(r, carry):
        sector = sector_of(lax.broadcasted_iota(I32, (R, STATES), 0) + r * R)
        a, b = lax.div(r, 4), mod4(r)
        for w in range(2):
            hi, low = halves(jnp.where(sector == targets[w], lg[r, w], 0.0))
            columns = slice(w * STATES, (w + 1) * STATES)
            m2[b, pl.ds(pl.multiple_of(a * R, 16), R), columns] = hi
            m2[b, pl.ds(pl.multiple_of(GROUP + a * R, 16), R), columns] = low
        return carry

    lax.fori_loop(0, 16, mask_rows, 0)

    rest_of(hf)
    to_group(3, hf)

    def rows_at(u, a, half):
        return q.at[u, pl.ds(pl.multiple_of(a * R + half * HALF, 8), HALF)]

    def half_of(ref, half):
        return ref.at[pl.ds(half * HALF, HALF)]

    def multiply(u):
        t, k = lax.div(u, 4), mod4(u)

        @pl.when(k == 0)
        def _():
            def one(w, carry):
                inner_tile(3, hf, w, t)
                return carry

            lax.fori_loop(0, 2, one, 0)

        o_h = mod4(h + step_of(k))
        both = dot(m2[o_h], ih[t], ROWS_NN)
        cross = dot(m2[o_h, :GROUP], il[t], ROWS_NN)
        q[u] = both[:GROUP] + both[GROUP:] + cross
        send(rows_at(u, yf, 0), far.at[u, 0], fs.at[u, 0], fr.at[u, 0], to_yp)
        send(rows_at(u, yf, 1), far.at[u, 1], fs.at[u, 1], fr.at[u, 1], to_ym)
        send(rows_at(u, yp, 1), half_of(near.at[u, 0], 1), ns.at[u, 0, 1], nr.at[u, 0, 1], to_yp)
        send(rows_at(u, ym, 0), half_of(near.at[u, 1], 0), ns.at[u, 1, 0], nr.at[u, 1, 0], to_ym)

    def pass_on(u):
        arrived(far.at[u, 0], fs.at[u, 0], fr.at[u, 0], to_yp)
        at = rows_at(u, yp, 0)
        at[...] = at[...] + far[u, 0]
        send(at, half_of(near.at[u, 0], 0), ns.at[u, 0, 0], nr.at[u, 0, 0], to_yp)
        arrived(far.at[u, 1], fs.at[u, 1], fr.at[u, 1], to_ym)
        at = rows_at(u, ym, 1)
        at[...] = at[...] + far[u, 1]
        send(at, half_of(near.at[u, 1], 1), ns.at[u, 1, 1], nr.at[u, 1, 1], to_ym)

    def total_along_y(u):
        t, k = lax.div(u, 4), mod4(u)
        for d in range(2):
            for half in range(2):
                arrived(half_of(near.at[u, d], half), ns.at[u, d, half], nr.at[u, d, half], to_yp)
        at = q.at[u, pl.ds(pl.multiple_of(y * R, 16), R)]
        at[...] = at[...] + near[u, 0] + near[u, 1]

        @pl.when(k == 0)
        def _():
            send(rows_at(u, y, 0), zfar.at[t, 0], zfs.at[t, 0], zfr.at[t, 0], to_hp)
            send(rows_at(u, y, 1), zfar.at[t, 1], zfs.at[t, 1], zfr.at[t, 1], to_hm)

        @pl.when(k == 1)
        def _():
            send(rows_at(u, y, 0), half_of(znear.at[t, 1], 0), zns.at[t, 1, 0], znr.at[t, 1, 0], to_hm)

        @pl.when(k == 2)
        def _():
            send(rows_at(u, y, 1), half_of(znear.at[t, 0], 1), zns.at[t, 0, 1], znr.at[t, 0, 1], to_hp)

        @pl.when(k == 3)
        def _():
            arrived(zfar.at[t, 0], zfs.at[t, 0], zfr.at[t, 0], to_hp)
            up = rows_at(u - 1, y, 0)
            up[...] = up[...] + zfar[t, 0]
            send(up, half_of(znear.at[t, 0], 0), zns.at[t, 0, 0], znr.at[t, 0, 0], to_hp)
            arrived(zfar.at[t, 1], zfs.at[t, 1], zfr.at[t, 1], to_hm)
            down = rows_at(u - 2, y, 1)
            down[...] = down[...] + zfar[t, 1]
            send(down, half_of(znear.at[t, 1], 1), zns.at[t, 1, 1], znr.at[t, 1, 1], to_hm)

    def total_along_z(t):
        for d in range(2):
            for half in range(2):
                arrived(half_of(znear.at[t, d], half), zns.at[t, d, half], znr.at[t, d, half], to_hp)
        mine = q[4 * t + 3, pl.ds(pl.multiple_of(y * R, 16), R)]
        out[:, pl.ds(pl.multiple_of(t * TILE, TILE), TILE)] = mine + znear[t, 0] + znear[t, 1]

    def scatter_step(s, carry):
        @pl.when(s < UNITS)
        def _():
            multiply(s)

        @pl.when((s >= LAG_FAR) & (s < UNITS + LAG_FAR))
        def _():
            pass_on(s - LAG_FAR)

        v = s - LAG_NEAR

        @pl.when(v >= 0)
        def _():
            total_along_y(v)

        @pl.when((v >= 6) & (mod4(v) == 2))
        def _():
            total_along_z(lax.div(v - 6, 4))

        return carry

    lax.fori_loop(0, UNITS + LAG_NEAR, scatter_step, 0)
    total_along_z(TILES - 1)

    def sent_out(ref, sem):
        pltpu.make_async_remote_copy(
            src_ref=ref, dst_ref=ref, send_sem=sem, recv_sem=sem, device_id=to_yp, device_id_type=MESH
        ).wait_send()

    def all_out(u, carry):
        for d in range(2):
            sent_out(far.at[u, d], fs.at[u, d])
            for half in range(2):
                sent_out(half_of(near.at[u, d], half), ns.at[u, d, half])
        return carry

    lax.fori_loop(0, UNITS, all_out, 0)
    for sems in (pzs, pys):
        for n in range(sems.shape[0]):
            sent_out(pg.at[0, pl.ds(0, HALF)], sems.at[n])
    for sems in (lls, lxs, lcs):
        for n in range(sems.shape[0]):
            sent_out(lg.at[0, 0], sems.at[n])
    for t in range(TILES):
        for d in range(2):
            sent_out(zfar.at[t, d], zfs.at[t, d])
            for half in range(2):
                sent_out(half_of(znear.at[t, d], half), zns.at[t, d, half])


def on_device(psi, left_env, right_env, sector_lengths, op_map):
    dma = pltpu.SemaphoreType.DMA
    anywhere = pl.BlockSpec(memory_space=pl.ANY)
    scalars = pl.BlockSpec(memory_space=pltpu.SMEM)
    return pl.pallas_call(
        kernel,
        out_shape=jax.ShapeDtypeStruct((R, BLOCK), F32),
        in_specs=[anywhere, anywhere, anywhere, scalars, scalars],
        out_specs=pl.BlockSpec(memory_space=pltpu.VMEM),
        scratch_shapes=[
            pltpu.VMEM((16, R, BLOCK), F32),
            pltpu.VMEM((16, 2, R, STATES), F32),
            pltpu.VMEM((2 * BLOCK, BLOCK), F32),
            pltpu.VMEM((2 * BLOCK, BLOCK), BF),
            pltpu.VMEM((2 * BLOCK, BLOCK), BF),
            pltpu.VMEM((4, 2 * GROUP, BLOCK), BF),
            pltpu.VMEM((TILES, 2 * STATES, TILE), BF),
            pltpu.VMEM((TILES, 2 * STATES, TILE), BF),
            pltpu.VMEM((4, 2 * GROUP, 2 * STATES), BF),
            pltpu.VMEM((UNITS, GROUP, TILE), F32),
            pltpu.VMEM((UNITS, 2, HALF, TILE), F32),
            pltpu.VMEM((UNITS, 2, R, TILE), F32),
            pltpu.VMEM((TILES, 2, HALF, TILE), F32),
            pltpu.VMEM((TILES, 2, R, TILE), F32),
            dma((3,)),
            dma((16, 2)), dma((6,)), dma((24,)),
            dma((16, 2)), dma((2,)), dma((12,)), dma((16,)),
            dma((UNITS, 2)), dma((UNITS, 2)), dma((UNITS, 2, 2)), dma((UNITS, 2, 2)),
            dma((TILES, 2)), dma((TILES, 2)), dma((TILES, 2, 2)), dma((TILES, 2, 2)),
        ],
        compiler_params=pltpu.CompilerParams(
            collective_id=0, has_side_effects=True, vmem_limit_bytes=60 * 1024 * 1024
        ),
    )(psi, left_env, right_env.reshape(2 * BLOCK, BLOCK), sector_lengths, op_map.T)


def solution(mesh):
    in_specs = (P("op", "right"), P("op", "right", None), P("op", "right", None), P(), P())
    return jax.shard_map(
        on_device, mesh=mesh, in_specs=in_specs, out_specs=P("op", "right"), check_vma=False
    )
```

```python
import jax
import jax.numpy as jnp
from jax import lax
from jax.experimental import pallas as pl
from jax.experimental.pallas import tpu as pltpu
from jax.sharding import PartitionSpec as P

MESH = pl.DeviceIdType.MESH
BF = jnp.bfloat16
F32 = jnp.float32
I32 = jnp.int32

R = 48
HALF = R // 2
STATES = 768
BLOCK = 1024
TILE = 256
TILES = BLOCK // TILE
GROUP = 4 * R
UNITS = 4 * TILES
LAG_FAR = 2
LAG_NEAR = 5
ROWS_NT = (((1,), (1,)), ((), ()))
ROWS_NN = (((1,), (0,)), ((), ()))


def mod4(v):
    return lax.rem(v, 4)


def dot(a, b, dims):
    return lax.dot_general(a, b, dims, preferred_element_type=F32)


def halves(v):
    hi = v.astype(BF)
    return hi, (v - hi.astype(F32)).astype(BF)


def step_of(k):
    return mod4(2 + k + lax.div(k * (k - 1), 2))


def kernel(
    psi, left, renv, lengths, op_map, out,
    pg, lg, raw, rh, rl, p2, early, ih, il, m2, q, far, near, zfar, znear,
    local_sem, prs, pzs, pys, lrs, lls, lxs, lcs, fs, fr, ns, nr, zfs, zfr, zns, znr,
):
    op, right = lax.axis_index("op"), lax.axis_index("right")
    y, h = lax.div(op, 4), mod4(op)
    l, x, c = lax.div(right, 8), mod4(lax.div(right, 2)), lax.rem(right, 2)
    yp, ym, yf = mod4(y + 1), mod4(y + 3), mod4(y + 2)
    hp, hm, hf = mod4(h + 1), mod4(h + 3), mod4(h + 2)
    xp, xm, xf = mod4(x + 1), mod4(x + 3), mod4(x + 2)
    lo = 1 - l

    def op_at(a, b):
        return a * 4 + b

    def right_at(a, b, d):
        return a * 8 + b * 2 + d

    to_yp, to_ym = (op_at(yp, h), right), (op_at(ym, h), right)
    to_hp, to_hm = (op_at(y, hp), right), (op_at(y, hm), right)
    to_xp, to_xm = (op, right_at(l, xp, c)), (op, right_at(l, xm, c))
    to_l, to_c = (op, right_at(lo, x, c)), (op, right_at(l, x, 1 - c))

    barrier = pltpu.get_barrier_semaphore()
    partners = (to_yp, to_ym, to_hp, to_hm, to_xp, to_xm, to_l, to_c)
    for device in partners:
        pl.semaphore_signal(barrier, inc=1, device_id=device, device_id_type=MESH)

    load_env = pltpu.make_async_copy(renv, raw, local_sem.at[0])
    load_psi = pltpu.make_async_copy(psi, pg.at[op], local_sem.at[1])
    load_left = pltpu.make_async_copy(left, lg.at[right], local_sem.at[2])
    load_psi.start()
    load_env.start()
    load_left.start()
    pl.semaphore_wait(barrier, len(partners))

    def send(src, dst, ssem, rsem, device):
        copy = pltpu.make_async_remote_copy(
            src_ref=src, dst_ref=dst, send_sem=ssem, recv_sem=rsem, device_id=device, device_id_type=MESH
        )
        copy.start()

    def arrived(dst, ssem, rsem, device):
        pltpu.make_async_remote_copy(
            src_ref=dst, dst_ref=dst, send_sem=ssem, recv_sem=rsem, device_id=device, device_id_type=MESH
        ).wait_recv()

    def piece(o, half):
        return pg.at[o, pl.ds(half * HALF, HALF)]

    counts = {"z": 0, "y": 0, "l": 0, "x": 0, "c": 0}
    psi_sems, left_sems = {"z": pzs, "y": pys}, {"l": lls, "x": lxs, "c": lcs}

    def psi_send(axis, o, half, device, src=None):
        sem = psi_sems[axis].at[counts[axis]]
        counts[axis] += 1
        dst = piece(o, half)
        send(dst if src is None else src.at[pl.ds(half * HALF, HALF)], dst, sem, prs.at[o, half], device)

    def psi_arrived(o, half):
        arrived(piece(o, half), pzs.at[0], prs.at[o, half], to_yp)

    def left_send(axis, r, w, device, src=None):
        sem = left_sems[axis].at[counts[axis]]
        counts[axis] += 1
        dst = lg.at[r, w]
        send(dst if src is None else src.at[w], dst, sem, lrs.at[r, w], device)

    def left_arrived(r, w):
        arrived(lg.at[r, w], lls.at[0], lrs.at[r, w], to_xp)

    psi_send("z", op, 0, to_hp, psi)
    psi_send("z", op, 1, to_hm, psi)
    psi_send("y", op, 0, to_yp, psi)
    psi_send("y", op, 1, to_ym, psi)
    psi_send("z", op, 1, to_hp, psi)
    psi_send("z", op, 0, to_hm, psi)
    psi_send("y", op, 1, to_yp, psi)
    psi_send("y", op, 0, to_ym, psi)
    for w in (0, 1):
        left_send("x", right, w, to_xp, left)
        left_send("x", right, 1 - w, to_xm, left)
    for w in (0, 1):
        left_send("c", right, w, to_c, left)

    def both_ways(o, half):
        psi_send("y", o, half, to_yp)
        psi_send("y", o, half, to_ym)

    def from_below(o_h):
        psi_arrived(op_at(ym, o_h), 0)
        psi_send("y", op_at(ym, o_h), 0, to_yp)

    def from_above(o_h):
        psi_arrived(op_at(yp, o_h), 1)
        psi_send("y", op_at(yp, o_h), 1, to_ym)

    def rest_of(o_h):
        psi_arrived(op_at(ym, o_h), 1)
        psi_arrived(op_at(yp, o_h), 0)
        psi_arrived(op_at(yf, o_h), 0)
        psi_arrived(op_at(yf, o_h), 1)

    def to_group(i, first, second):
        for a in range(4):
            rows = jnp.concatenate([pg[op_at(a, first), :HALF], pg[op_at(a, second), HALF:]], axis=0)
            hi, low = halves(rows)
            p2[i, a * R:(a + 1) * R] = hi
            p2[i, GROUP + a * R:GROUP + (a + 1) * R] = low

    def left_on(r, w):
        left_arrived(r, w)
        left_send("c", r, w, to_c)

    def inner_tile(i, w, t):
        rows = pl.ds(pl.multiple_of(w * BLOCK + t * TILE, TILE), TILE)
        both = dot(p2[i], rh[rows, :], ROWS_NT)
        cross = dot(p2[i, :GROUP], rl[rows, :], ROWS_NT)
        return both[:GROUP] + both[GROUP:] + cross

    def keep_inner(v, o_h, w, t):
        hi, low = halves(v)
        for a in range(4):
            at = pl.ds(pl.multiple_of(w * STATES + op_at(a, o_h) * R, 16), R)
            ih[t, at, :] = hi[a * R:(a + 1) * R]
            il[t, at, :] = low[a * R:(a + 1) * R]

    load_env.wait()

    def split_env(s, carry):
        rows = pl.ds(pl.multiple_of(s * 32, 32), 32)
        hi, low = halves(raw[rows, :])
        rh[rows, :] = hi
        rl[rows, :] = low
        return carry

    lax.fori_loop(0, 2 * BLOCK // 32, split_env, 0)
    load_psi.wait()

    from_below(h)
    from_above(h)
    psi_arrived(op_at(y, hm), 0)
    psi_send("z", op_at(y, hm), 0, to_hp)
    both_ways(op_at(y, hm), 0)
    psi_arrived(op_at(y, hp), 1)
    psi_send("z", op_at(y, hp), 1, to_hm)
    both_ways(op_at(y, hp), 1)
    left_send("l", right, 0, to_l, left)
    left_send("l", right, 1, to_l, left)
    left_arrived(right_at(l, xm, c), 0)
    left_send("x", right_at(l, xm, c), 0, to_xp)
    left_send("c", right_at(l, xm, c), 0, to_c)
    left_arrived(right_at(l, xp, c), 1)
    left_send("x", right_at(l, xp, c), 1, to_xm)
    left_send("c", right_at(l, xp, c), 1, to_c)
    rest_of(h)
    to_group(0, h, h)

    def second_halves():
        psi_arrived(op_at(y, hp), 0)
        both_ways(op_at(y, hp), 0)
        psi_arrived(op_at(y, hm), 1)
        both_ways(op_at(y, hm), 1)

    def first_pairs():
        for o_h, half in ((hm, 0), (hp, 1)):
            psi_arrived(op_at(ym if half else yp, o_h), half)
            psi_arrived(op_at(yf, o_h), half)
        to_group(1, hm, hp)

    def second_pairs():
        for o_h, half in ((hp, 0), (hm, 1)):
            psi_arrived(op_at(ym if half else yp, o_h), half)
            psi_arrived(op_at(yf, o_h), half)
        to_group(2, hp, hm)

    def farthest(half):
        psi_arrived(op_at(y, hf), half)
        both_ways(op_at(y, hf), half)

    def left_across(w):
        r = right_at(lo, x, c)
        left_arrived(r, w)
        left_send("x", r, w, to_xp)
        left_send("x", r, w, to_xm)
        left_send("c", r, w, to_c)

    def left_turn():
        r = right_at(lo, xm, c)
        left_arrived(r, 0)
        left_send("x", r, 0, to_xp)
        left_send("c", r, 0, to_c)
        r = right_at(lo, xp, c)
        left_arrived(r, 1)
        left_send("x", r, 1, to_xm)
        left_send("c", r, 1, to_c)

    def left_pair(a, b, second):
        left_on(right_at(a, b[0], c), second[0])
        left_on(right_at(a, b[1], c), second[1])

    events = {
        3: [(left_pair, l, (xm, xp), (1, 0))],
        4: [(second_halves,)],
        5: [(from_above, hp), (from_below, hm)],
        7: [(left_pair, l, (xf, xf), (0, 1))],
        8: [
            (farthest, 0), (farthest, 1), (left_across, 0), (from_below, hp), (from_above, hm),
            (left_across, 1), (first_pairs,),
        ],
        11: [(left_turn,)],
        13: [(from_below, hf), (from_above, hf)],
        16: [(second_pairs,)],
        18: [(left_pair, lo, (xm, xp), (1, 0))],
        22: [(left_pair, lo, (xf, xf), (0, 1))],
    }

    def gather_step(e, carry):
        for at, calls in events.items():
            @pl.when(e == at)
            def _(calls=calls):
                for call, *rest in calls:
                    call(*rest)

        i, n = lax.div(e, 8), lax.rem(e, 8)
        w, t = lax.div(n, 4), mod4(n)
        v = inner_tile(i, w, t)

        @pl.when(i == 0)
        def _():
            keep_inner(v, h, w, t)

        @pl.when(i == 1)
        def _():
            early[n] = v

        @pl.when(i == 2)
        def _():
            before = early[n]
            first = lax.rem(lax.broadcasted_iota(I32, (GROUP, TILE), 0), R) < HALF
            keep_inner(jnp.where(first, before, v), hm, w, t)
            keep_inner(jnp.where(first, v, before), hp, w, t)

        return carry

    lax.fori_loop(0, 24, gather_step, 0)

    load_left.wait()
    for a in range(2):
        for b in range(4):
            for w in range(2):
                left_arrived(right_at(a, b, 1 - c), w)

    ends = []
    total = 0
    for k in range(4):
        total = total + lengths[k]
        ends.append(total)

    def sector_of(place):
        s = jnp.zeros(place.shape, I32)
        for end in ends:
            s = s + (place >= end).astype(I32)
        return s

    column_sector = sector_of(lax.broadcasted_iota(I32, (R, STATES), 1))
    targets = []
    for w in range(2):
        target = jnp.full((R, STATES), -1, I32)
        for k in range(4):
            target = jnp.where(column_sector == k, op_map[k, 2 * op + w], target)
        targets.append(target)

    def mask_rows(r, carry):
        sector = sector_of(lax.broadcasted_iota(I32, (R, STATES), 0) + r * R)
        a, b = lax.div(r, 4), mod4(r)
        for w in range(2):
            hi, low = halves(jnp.where(sector == targets[w], lg[r, w], 0.0))
            columns = slice(w * STATES, (w + 1) * STATES)
            m2[b, pl.ds(pl.multiple_of(a * R, 16), R), columns] = hi
            m2[b, pl.ds(pl.multiple_of(GROUP + a * R, 16), R), columns] = low
        return carry

    lax.fori_loop(0, 16, mask_rows, 0)

    rest_of(hf)
    to_group(3, hf, hf)

    def rows_at(u, a, half):
        return q.at[u, pl.ds(pl.multiple_of(a * R + half * HALF, 8), HALF)]

    def half_of(ref, half):
        return ref.at[pl.ds(half * HALF, HALF)]

    def place_of(u):
        late = lax.div(u, 2 * TILES)
        k = (1 - late) * lax.rem(u, 2) + late * lax.div(u, TILES)
        t = (1 - late) * lax.div(u, 2) + late * lax.rem(u, TILES)
        return k, t

    def multiply(u):
        k, t = place_of(u)

        @pl.when(k == 0)
        def _():
            def one(w, carry):
                keep_inner(inner_tile(3, w, t), hf, w, t)
                return carry

            lax.fori_loop(0, 2, one, 0)

        o_h = mod4(h + step_of(k))
        both = dot(m2[o_h], ih[t], ROWS_NN)
        cross = dot(m2[o_h, :GROUP], il[t], ROWS_NN)
        q[u] = both[:GROUP] + both[GROUP:] + cross
        send(rows_at(u, yf, 0), far.at[u, 0], fs.at[u, 0], fr.at[u, 0], to_yp)
        send(rows_at(u, yf, 1), far.at[u, 1], fs.at[u, 1], fr.at[u, 1], to_ym)
        send(rows_at(u, yp, 1), half_of(near.at[u, 0], 1), ns.at[u, 0, 1], nr.at[u, 0, 1], to_yp)
        send(rows_at(u, ym, 0), half_of(near.at[u, 1], 0), ns.at[u, 1, 0], nr.at[u, 1, 0], to_ym)

    def pass_on(u):
        arrived(far.at[u, 0], fs.at[u, 0], fr.at[u, 0], to_yp)
        at = rows_at(u, yp, 0)
        at[...] = at[...] + far[u, 0]
        send(at, half_of(near.at[u, 0], 0), ns.at[u, 0, 0], nr.at[u, 0, 0], to_yp)
        arrived(far.at[u, 1], fs.at[u, 1], fr.at[u, 1], to_ym)
        at = rows_at(u, ym, 1)
        at[...] = at[...] + far[u, 1]
        send(at, half_of(near.at[u, 1], 1), ns.at[u, 1, 1], nr.at[u, 1, 1], to_ym)

    def total_along_y(u):
        k, t = place_of(u)
        for d in range(2):
            for half in range(2):
                arrived(half_of(near.at[u, d], half), ns.at[u, d, half], nr.at[u, d, half], to_yp)
        at = q.at[u, pl.ds(pl.multiple_of(y * R, 16), R)]
        at[...] = at[...] + near[u, 0] + near[u, 1]

        @pl.when(k == 0)
        def _():
            send(rows_at(u, y, 0), zfar.at[t, 0], zfs.at[t, 0], zfr.at[t, 0], to_hp)
            send(rows_at(u, y, 1), zfar.at[t, 1], zfs.at[t, 1], zfr.at[t, 1], to_hm)

        @pl.when(k == 1)
        def _():
            send(rows_at(u, y, 0), half_of(znear.at[t, 1], 0), zns.at[t, 1, 0], znr.at[t, 1, 0], to_hm)

        @pl.when(k == 2)
        def _():
            send(rows_at(u, y, 1), half_of(znear.at[t, 0], 1), zns.at[t, 0, 1], znr.at[t, 0, 1], to_hp)
            arrived(zfar.at[t, 1], zfs.at[t, 1], zfr.at[t, 1], to_hm)
            down = rows_at(2 * t + 1, y, 1)
            down[...] = down[...] + zfar[t, 1]
            send(down, half_of(znear.at[t, 1], 1), zns.at[t, 1, 1], znr.at[t, 1, 1], to_hm)
            arrived(zfar.at[t, 0], zfs.at[t, 0], zfr.at[t, 0], to_hp)
            up = rows_at(u, y, 0)
            up[...] = up[...] + zfar[t, 0]
            send(up, half_of(znear.at[t, 0], 0), zns.at[t, 0, 0], znr.at[t, 0, 0], to_hp)

        @pl.when(k == 3)
        def _():
            for d in range(2):
                for half in range(2):
                    arrived(half_of(znear.at[t, d], half), zns.at[t, d, half], znr.at[t, d, half], to_hp)
            out[:, pl.ds(pl.multiple_of(t * TILE, TILE), TILE)] = at[...] + znear[t, 0] + znear[t, 1]

    def scatter_step(s, carry):
        @pl.when(s < UNITS)
        def _():
            multiply(s)

        @pl.when((s >= LAG_FAR) & (s < UNITS + LAG_FAR))
        def _():
            pass_on(s - LAG_FAR)

        v = s - LAG_NEAR

        @pl.when(v >= 0)
        def _():
            total_along_y(v)

        return carry

    lax.fori_loop(0, UNITS + LAG_NEAR, scatter_step, 0)

    def sent_out(ref, sem):
        pltpu.make_async_remote_copy(
            src_ref=ref, dst_ref=ref, send_sem=sem, recv_sem=sem, device_id=to_yp, device_id_type=MESH
        ).wait_send()

    def all_out(u, carry):
        for d in range(2):
            sent_out(far.at[u, d], fs.at[u, d])
            for half in range(2):
                sent_out(half_of(near.at[u, d], half), ns.at[u, d, half])
        return carry

    lax.fori_loop(0, UNITS, all_out, 0)
    for sems in (pzs, pys):
        for n in range(sems.shape[0]):
            sent_out(pg.at[0, pl.ds(0, HALF)], sems.at[n])
    for sems in (lls, lxs, lcs):
        for n in range(sems.shape[0]):
            sent_out(lg.at[0, 0], sems.at[n])
    for t in range(TILES):
        for d in range(2):
            sent_out(zfar.at[t, d], zfs.at[t, d])
            for half in range(2):
                sent_out(half_of(znear.at[t, d], half), zns.at[t, d, half])


def on_device(psi, left_env, right_env, sector_lengths, op_map):
    dma = pltpu.SemaphoreType.DMA
    anywhere = pl.BlockSpec(memory_space=pl.ANY)
    scalars = pl.BlockSpec(memory_space=pltpu.SMEM)
    return pl.pallas_call(
        kernel,
        out_shape=jax.ShapeDtypeStruct((R, BLOCK), F32),
        in_specs=[anywhere, anywhere, anywhere, scalars, scalars],
        out_specs=pl.BlockSpec(memory_space=pltpu.VMEM),
        scratch_shapes=[
            pltpu.VMEM((16, R, BLOCK), F32),
            pltpu.VMEM((16, 2, R, STATES), F32),
            pltpu.VMEM((2 * BLOCK, BLOCK), F32),
            pltpu.VMEM((2 * BLOCK, BLOCK), BF),
            pltpu.VMEM((2 * BLOCK, BLOCK), BF),
            pltpu.VMEM((4, 2 * GROUP, BLOCK), BF),
            pltpu.VMEM((2 * TILES, GROUP, TILE), F32),
            pltpu.VMEM((TILES, 2 * STATES, TILE), BF),
            pltpu.VMEM((TILES, 2 * STATES, TILE), BF),
            pltpu.VMEM((4, 2 * GROUP, 2 * STATES), BF),
            pltpu.VMEM((UNITS, GROUP, TILE), F32),
            pltpu.VMEM((UNITS, 2, HALF, TILE), F32),
            pltpu.VMEM((UNITS, 2, R, TILE), F32),
            pltpu.VMEM((TILES, 2, HALF, TILE), F32),
            pltpu.VMEM((TILES, 2, R, TILE), F32),
            dma((3,)),
            dma((16, 2)), dma((6,)), dma((24,)),
            dma((16, 2)), dma((2,)), dma((12,)), dma((16,)),
            dma((UNITS, 2)), dma((UNITS, 2)), dma((UNITS, 2, 2)), dma((UNITS, 2, 2)),
            dma((TILES, 2)), dma((TILES, 2)), dma((TILES, 2, 2)), dma((TILES, 2, 2)),
        ],
        compiler_params=pltpu.CompilerParams(
            collective_id=0, has_side_effects=True, vmem_limit_bytes=60 * 1024 * 1024
        ),
    )(psi, left_env, right_env.reshape(2 * BLOCK, BLOCK), sector_lengths, op_map.T)


def solution(mesh):
    in_specs = (P("op", "right"), P("op", "right", None), P("op", "right", None), P(), P())
    return jax.shard_map(
        on_device, mesh=mesh, in_specs=in_specs, out_specs=P("op", "right"), check_vma=False
    )
```

```python
import jax
import jax.numpy as jnp
from jax import lax
from jax.experimental import pallas as pl
from jax.experimental.pallas import tpu as pltpu
from jax.sharding import PartitionSpec as P

MESH = pl.DeviceIdType.MESH
BF = jnp.bfloat16
F32 = jnp.float32
I32 = jnp.int32

R = 48
HALF = R // 2
STATES = 768
BLOCK = 1024
TILE = 256
TILES = BLOCK // TILE
GROUP = 4 * R
UNITS = 4 * TILES
LAG_FAR = 4
LAG_NEAR = 8
ROWS_NT = (((1,), (1,)), ((), ()))
ROWS_NN = (((1,), (0,)), ((), ()))


def mod4(v):
    return lax.rem(v, 4)


def dot(a, b, dims):
    return lax.dot_general(a, b, dims, preferred_element_type=F32)


def halves(v):
    hi = v.astype(BF)
    return hi, (v - hi.astype(F32)).astype(BF)


def step_of(k):
    return mod4(2 + k + lax.div(k * (k - 1), 2))


def kernel(
    psi, left, renv, lengths, op_map, out,
    pg, lg, raw, rh, rl, p2, last, early, ih, il, m2, q, far, near, zfar, znear,
    local_sem, prs, pzs, pys, lrs, lls, lxs, lcs, fs, fr, ns, nr, zfs, zfr, zns, znr,
):
    op, right = lax.axis_index("op"), lax.axis_index("right")
    y, h = lax.div(op, 4), mod4(op)
    l, x, c = lax.div(right, 8), mod4(lax.div(right, 2)), lax.rem(right, 2)
    yp, ym, yf = mod4(y + 1), mod4(y + 3), mod4(y + 2)
    hp, hm, hf = mod4(h + 1), mod4(h + 3), mod4(h + 2)
    xp, xm, xf = mod4(x + 1), mod4(x + 3), mod4(x + 2)
    lo = 1 - l

    def op_at(a, b):
        return a * 4 + b

    def right_at(a, b, d):
        return a * 8 + b * 2 + d

    to_yp, to_ym = (op_at(yp, h), right), (op_at(ym, h), right)
    to_hp, to_hm = (op_at(y, hp), right), (op_at(y, hm), right)
    to_xp, to_xm = (op, right_at(l, xp, c)), (op, right_at(l, xm, c))
    to_l, to_c = (op, right_at(lo, x, c)), (op, right_at(l, x, 1 - c))

    barrier = pltpu.get_barrier_semaphore()
    partners = (to_yp, to_ym, to_hp, to_hm, to_xp, to_xm, to_l, to_c)
    for device in partners:
        pl.semaphore_signal(barrier, inc=1, device_id=device, device_id_type=MESH)

    load_env = pltpu.make_async_copy(renv, raw, local_sem.at[0])
    load_psi = pltpu.make_async_copy(psi, pg.at[op], local_sem.at[1])
    load_left = pltpu.make_async_copy(left, lg.at[right], local_sem.at[2])
    load_psi.start()
    load_env.start()
    load_left.start()
    pl.semaphore_wait(barrier, len(partners))

    def send(src, dst, ssem, rsem, device):
        copy = pltpu.make_async_remote_copy(
            src_ref=src, dst_ref=dst, send_sem=ssem, recv_sem=rsem, device_id=device, device_id_type=MESH
        )
        copy.start()

    def arrived(dst, ssem, rsem, device):
        pltpu.make_async_remote_copy(
            src_ref=dst, dst_ref=dst, send_sem=ssem, recv_sem=rsem, device_id=device, device_id_type=MESH
        ).wait_recv()

    def piece(o, half):
        return pg.at[o, pl.ds(half * HALF, HALF)]

    counts = {"z": 0, "y": 0, "l": 0, "x": 0, "c": 0}
    psi_sems, left_sems = {"z": pzs, "y": pys}, {"l": lls, "x": lxs, "c": lcs}

    def psi_send(axis, o, half, device, src=None):
        sem = psi_sems[axis].at[counts[axis]]
        counts[axis] += 1
        dst = piece(o, half)
        send(dst if src is None else src.at[pl.ds(half * HALF, HALF)], dst, sem, prs.at[o, half], device)

    def psi_arrived(o, half):
        arrived(piece(o, half), pzs.at[0], prs.at[o, half], to_yp)

    def left_send(axis, r, w, device, src=None):
        sem = left_sems[axis].at[counts[axis]]
        counts[axis] += 1
        dst = lg.at[r, w]
        send(dst if src is None else src.at[w], dst, sem, lrs.at[r, w], device)

    def left_arrived(r, w):
        arrived(lg.at[r, w], lls.at[0], lrs.at[r, w], to_xp)

    psi_send("z", op, 0, to_hp, psi)
    psi_send("z", op, 1, to_hm, psi)
    psi_send("y", op, 0, to_yp, psi)
    psi_send("y", op, 1, to_ym, psi)
    psi_send("z", op, 1, to_hp, psi)
    psi_send("z", op, 0, to_hm, psi)
    psi_send("y", op, 1, to_yp, psi)
    psi_send("y", op, 0, to_ym, psi)
    for w in (0, 1):
        left_send("x", right, w, to_xp, left)
        left_send("x", right, 1 - w, to_xm, left)
    for w in (0, 1):
        left_send("c", right, w, to_c, left)

    def both_ways(o, half):
        psi_send("y", o, half, to_yp)
        psi_send("y", o, half, to_ym)

    def from_below(o_h):
        psi_arrived(op_at(ym, o_h), 0)
        psi_send("y", op_at(ym, o_h), 0, to_yp)

    def from_above(o_h):
        psi_arrived(op_at(yp, o_h), 1)
        psi_send("y", op_at(yp, o_h), 1, to_ym)

    def rest_of(o_h):
        psi_arrived(op_at(ym, o_h), 1)
        psi_arrived(op_at(yp, o_h), 0)
        psi_arrived(op_at(yf, o_h), 0)
        psi_arrived(op_at(yf, o_h), 1)

    def to_group(ref, size, at, first, second):
        for a in range(4):
            rows = jnp.concatenate([pg[op_at(a, first), :HALF], pg[op_at(a, second), HALF:]], axis=0)
            hi, low = halves(rows)
            ref[at + a * R:at + (a + 1) * R] = hi
            ref[size + at + a * R:size + at + (a + 1) * R] = low

    def left_on(r, w):
        left_arrived(r, w)
        left_send("c", r, w, to_c)

    def inner_tile(ref, size, w, t):
        rows = pl.ds(pl.multiple_of(w * BLOCK + t * TILE, TILE), TILE)
        both = dot(ref[...], rh[rows, :], ROWS_NT)
        cross = dot(ref[:size], rl[rows, :], ROWS_NT)
        return both[:size] + both[size:] + cross

    def keep_inner(v, o_h, w, t):
        hi, low = halves(v)
        for a in range(4):
            at = pl.ds(pl.multiple_of(w * STATES + op_at(a, o_h) * R, 16), R)
            ih[t, at, :] = hi[a * R:(a + 1) * R]
            il[t, at, :] = low[a * R:(a + 1) * R]

    ends = []
    total = 0
    for k in range(4):
        total = total + lengths[k]
        ends.append(total)

    def sector_of(place):
        s = jnp.zeros(place.shape, I32)
        for end in ends:
            s = s + (place >= end).astype(I32)
        return s

    column_sector = sector_of(lax.broadcasted_iota(I32, (R, STATES), 1))
    targets = []
    for w in range(2):
        target = jnp.full((R, STATES), -1, I32)
        for k in range(4):
            target = jnp.where(column_sector == k, op_map[k, 2 * op + w], target)
        targets.append(target)

    def mask_from(side):
        for b in range(4):
            for w in range(2):
                left_arrived(right_at(side, b, 1 - c), w)

        def mask_rows(n, carry):
            r = side * 8 + n
            sector = sector_of(lax.broadcasted_iota(I32, (R, STATES), 0) + r * R)
            a, b = lax.div(r, 4), mod4(r)
            for w in range(2):
                hi, low = halves(jnp.where(sector == targets[w], lg[r, w], 0.0))
                columns = slice(w * STATES, (w + 1) * STATES)
                m2[b, pl.ds(pl.multiple_of(a * R, 16), R), columns] = hi
                m2[b, pl.ds(pl.multiple_of(GROUP + a * R, 16), R), columns] = low
            return carry

        lax.fori_loop(0, 8, mask_rows, 0)

    load_env.wait()

    def split_env(s, carry):
        rows = pl.ds(pl.multiple_of(s * 32, 32), 32)
        hi, low = halves(raw[rows, :])
        rh[rows, :] = hi
        rl[rows, :] = low
        return carry

    lax.fori_loop(0, 2 * BLOCK // 32, split_env, 0)
    load_psi.wait()
    load_left.wait()

    from_below(h)
    from_above(h)
    psi_arrived(op_at(y, hm), 0)
    psi_send("z", op_at(y, hm), 0, to_hp)
    both_ways(op_at(y, hm), 0)
    psi_arrived(op_at(y, hp), 1)
    psi_send("z", op_at(y, hp), 1, to_hm)
    both_ways(op_at(y, hp), 1)
    left_send("l", right, 0, to_l, left)
    left_send("l", right, 1, to_l, left)
    left_arrived(right_at(l, xm, c), 0)
    left_send("x", right_at(l, xm, c), 0, to_xp)
    left_send("c", right_at(l, xm, c), 0, to_c)
    left_arrived(right_at(l, xp, c), 1)
    left_send("x", right_at(l, xp, c), 1, to_xm)
    left_send("c", right_at(l, xp, c), 1, to_c)
    rest_of(h)
    to_group(p2.at[0], GROUP, 0, h, h)

    def second_halves():
        psi_arrived(op_at(y, hp), 0)
        both_ways(op_at(y, hp), 0)
        psi_arrived(op_at(y, hm), 1)
        both_ways(op_at(y, hm), 1)

    def first_pairs():
        for o_h, half in ((hm, 0), (hp, 1)):
            psi_arrived(op_at(ym if half else yp, o_h), half)
            psi_arrived(op_at(yf, o_h), half)
        to_group(p2.at[1], GROUP, 0, hm, hp)

    def second_pairs():
        for o_h, half in ((hp, 0), (hm, 1)):
            psi_arrived(op_at(ym if half else yp, o_h), half)
            psi_arrived(op_at(yf, o_h), half)
        to_group(last, 2 * GROUP, 0, hp, hm)

    def farthest(half):
        psi_arrived(op_at(y, hf), half)
        both_ways(op_at(y, hf), half)

    def left_across(w):
        r = right_at(lo, x, c)
        left_arrived(r, w)
        left_send("x", r, w, to_xp)
        left_send("x", r, w, to_xm)
        left_send("c", r, w, to_c)

    def left_turn():
        r = right_at(lo, xm, c)
        left_arrived(r, 0)
        left_send("x", r, 0, to_xp)
        left_send("c", r, 0, to_c)
        r = right_at(lo, xp, c)
        left_arrived(r, 1)
        left_send("x", r, 1, to_xm)
        left_send("c", r, 1, to_c)

    def left_pair(a, b, second):
        left_on(right_at(a, b[0], c), second[0])
        left_on(right_at(a, b[1], c), second[1])

    events = {
        3: [(left_pair, l, (xm, xp), (1, 0))],
        4: [(second_halves,)],
        5: [(from_above, hp), (from_below, hm)],
        7: [(left_pair, l, (xf, xf), (0, 1))],
        8: [
            (farthest, 0), (farthest, 1), (left_across, 0), (from_below, hp), (from_above, hm),
            (left_across, 1), (mask_from, l), (first_pairs,),
        ],
        11: [(left_turn,)],
        13: [(from_below, hf), (from_above, hf)],
    }

    def gather_step(e, carry):
        for at, calls in events.items():
            @pl.when(e == at)
            def _(calls=calls):
                for call, *rest in calls:
                    call(*rest)

        i, n = lax.div(e, 8), lax.rem(e, 8)
        w, t = lax.div(n, 4), mod4(n)
        v = inner_tile(p2.at[i], GROUP, w, t)

        @pl.when(i == 0)
        def _():
            keep_inner(v, h, w, t)

        @pl.when(i == 1)
        def _():
            early[n] = v

        return carry

    lax.fori_loop(0, 16, gather_step, 0)
    second_pairs()
    left_pair(lo, (xm, xp), (1, 0))
    left_pair(lo, (xf, xf), (0, 1))

    mask_from(lo)

    rest_of(hf)
    to_group(last, 2 * GROUP, GROUP, hf, hf)

    def rows_at(u, a, half):
        return q.at[u, pl.ds(pl.multiple_of(a * R + half * HALF, 8), HALF)]

    def half_of(ref, half):
        return ref.at[pl.ds(half * HALF, HALF)]

    def place_of(u):
        late = lax.div(u, 3 * TILES)
        k = (1 - late) * lax.rem(u, 3) + late * 3
        t = (1 - late) * lax.div(u, 3) + late * lax.rem(u, 3 * TILES)
        return k, t

    def multiply(u):
        k, t = place_of(u)

        @pl.when(k == 0)
        def _():
            def one(w, carry):
                v = inner_tile(last, 2 * GROUP, w, t)
                keep_inner(v[GROUP:], hf, w, t)
                before, after = early[w * TILES + t], v[:GROUP]
                first = lax.rem(lax.broadcasted_iota(I32, (GROUP, TILE), 0), R) < HALF
                keep_inner(jnp.where(first, before, after), hm, w, t)
                keep_inner(jnp.where(first, after, before), hp, w, t)
                return carry

            lax.fori_loop(0, 2, one, 0)

        o_h = mod4(h + step_of(k))
        both = dot(m2[o_h], ih[t], ROWS_NN)
        cross = dot(m2[o_h, :GROUP], il[t], ROWS_NN)
        q[u] = both[:GROUP] + both[GROUP:] + cross
        send(rows_at(u, yf, 0), far.at[u, 0], fs.at[u, 0], fr.at[u, 0], to_yp)
        send(rows_at(u, yf, 1), far.at[u, 1], fs.at[u, 1], fr.at[u, 1], to_ym)
        send(rows_at(u, yp, 1), half_of(near.at[u, 0], 1), ns.at[u, 0, 1], nr.at[u, 0, 1], to_yp)
        send(rows_at(u, ym, 0), half_of(near.at[u, 1], 0), ns.at[u, 1, 0], nr.at[u, 1, 0], to_ym)

    def pass_on(u):
        arrived(far.at[u, 0], fs.at[u, 0], fr.at[u, 0], to_yp)
        at = rows_at(u, yp, 0)
        at[...] = at[...] + far[u, 0]
        send(at, half_of(near.at[u, 0], 0), ns.at[u, 0, 0], nr.at[u, 0, 0], to_yp)
        arrived(far.at[u, 1], fs.at[u, 1], fr.at[u, 1], to_ym)
        at = rows_at(u, ym, 1)
        at[...] = at[...] + far[u, 1]
        send(at, half_of(near.at[u, 1], 1), ns.at[u, 1, 1], nr.at[u, 1, 1], to_ym)

    def pass_on_z(t):
        arrived(zfar.at[t, 1], zfs.at[t, 1], zfr.at[t, 1], to_hm)
        down = rows_at(3 * t + 1, y, 1)
        down[...] = down[...] + zfar[t, 1]
        send(down, half_of(znear.at[t, 1], 1), zns.at[t, 1, 1], znr.at[t, 1, 1], to_hm)
        arrived(zfar.at[t, 0], zfs.at[t, 0], zfr.at[t, 0], to_hp)
        up = rows_at(3 * t + 2, y, 0)
        up[...] = up[...] + zfar[t, 0]
        send(up, half_of(znear.at[t, 0], 0), zns.at[t, 0, 0], znr.at[t, 0, 0], to_hp)

    def total_along_y(u):
        k, t = place_of(u)
        for d in range(2):
            for half in range(2):
                arrived(half_of(near.at[u, d], half), ns.at[u, d, half], nr.at[u, d, half], to_yp)
        at = q.at[u, pl.ds(pl.multiple_of(y * R, 16), R)]
        at[...] = at[...] + near[u, 0] + near[u, 1]

        @pl.when(k == 0)
        def _():
            send(rows_at(u, y, 0), zfar.at[t, 0], zfs.at[t, 0], zfr.at[t, 0], to_hp)
            send(rows_at(u, y, 1), zfar.at[t, 1], zfs.at[t, 1], zfr.at[t, 1], to_hm)

        @pl.when(k == 1)
        def _():
            send(rows_at(u, y, 0), half_of(znear.at[t, 1], 0), zns.at[t, 1, 0], znr.at[t, 1, 0], to_hm)

        @pl.when(k == 2)
        def _():
            send(rows_at(u, y, 1), half_of(znear.at[t, 0], 1), zns.at[t, 0, 1], znr.at[t, 0, 1], to_hp)

        @pl.when(k == 3)
        def _():
            for d in range(2):
                for half in range(2):
                    arrived(half_of(znear.at[t, d], half), zns.at[t, d, half], znr.at[t, d, half], to_hp)
            out[:, pl.ds(pl.multiple_of(t * TILE, TILE), TILE)] = at[...] + znear[t, 0] + znear[t, 1]

    def scatter_step(s, carry):
        @pl.when(s < UNITS)
        def _():
            multiply(s)

        @pl.when((s >= LAG_FAR) & (s < UNITS + LAG_FAR))
        def _():
            pass_on(s - LAG_FAR)

        v = s - LAG_NEAR

        @pl.when((v >= 3) & (v <= 3 * TILES) & (lax.rem(v, 3) == 0))
        def _():
            pass_on_z(lax.div(v, 3) - 1)

        @pl.when(v >= 0)
        def _():
            total_along_y(v)

        return carry

    lax.fori_loop(0, UNITS + LAG_NEAR, scatter_step, 0)

    def sent_out(ref, sem):
        pltpu.make_async_remote_copy(
            src_ref=ref, dst_ref=ref, send_sem=sem, recv_sem=sem, device_id=to_yp, device_id_type=MESH
        ).wait_send()

    def all_out(u, carry):
        for d in range(2):
            sent_out(far.at[u, d], fs.at[u, d])
            for half in range(2):
                sent_out(half_of(near.at[u, d], half), ns.at[u, d, half])
        return carry

    lax.fori_loop(0, UNITS, all_out, 0)
    for sems in (pzs, pys):
        for n in range(sems.shape[0]):
            sent_out(pg.at[0, pl.ds(0, HALF)], sems.at[n])
    for sems in (lls, lxs, lcs):
        for n in range(sems.shape[0]):
            sent_out(lg.at[0, 0], sems.at[n])
    for t in range(TILES):
        for d in range(2):
            sent_out(zfar.at[t, d], zfs.at[t, d])
            for half in range(2):
                sent_out(half_of(znear.at[t, d], half), zns.at[t, d, half])


def on_device(psi, left_env, right_env, sector_lengths, op_map):
    dma = pltpu.SemaphoreType.DMA
    anywhere = pl.BlockSpec(memory_space=pl.ANY)
    scalars = pl.BlockSpec(memory_space=pltpu.SMEM)
    return pl.pallas_call(
        kernel,
        out_shape=jax.ShapeDtypeStruct((R, BLOCK), F32),
        in_specs=[anywhere, anywhere, anywhere, scalars, scalars],
        out_specs=pl.BlockSpec(memory_space=pltpu.VMEM),
        scratch_shapes=[
            pltpu.VMEM((16, R, BLOCK), F32),
            pltpu.VMEM((16, 2, R, STATES), F32),
            pltpu.VMEM((2 * BLOCK, BLOCK), F32),
            pltpu.VMEM((2 * BLOCK, BLOCK), BF),
            pltpu.VMEM((2 * BLOCK, BLOCK), BF),
            pltpu.VMEM((2, 2 * GROUP, BLOCK), BF),
            pltpu.VMEM((4 * GROUP, BLOCK), BF),
            pltpu.VMEM((2 * TILES, GROUP, TILE), F32),
            pltpu.VMEM((TILES, 2 * STATES, TILE), BF),
            pltpu.VMEM((TILES, 2 * STATES, TILE), BF),
            pltpu.VMEM((4, 2 * GROUP, 2 * STATES), BF),
            pltpu.VMEM((UNITS, GROUP, TILE), F32),
            pltpu.VMEM((UNITS, 2, HALF, TILE), F32),
            pltpu.VMEM((UNITS, 2, R, TILE), F32),
            pltpu.VMEM((TILES, 2, HALF, TILE), F32),
            pltpu.VMEM((TILES, 2, R, TILE), F32),
            dma((3,)),
            dma((16, 2)), dma((6,)), dma((24,)),
            dma((16, 2)), dma((2,)), dma((12,)), dma((16,)),
            dma((UNITS, 2)), dma((UNITS, 2)), dma((UNITS, 2, 2)), dma((UNITS, 2, 2)),
            dma((TILES, 2)), dma((TILES, 2)), dma((TILES, 2, 2)), dma((TILES, 2, 2)),
        ],
        compiler_params=pltpu.CompilerParams(
            collective_id=0, has_side_effects=True, vmem_limit_bytes=60 * 1024 * 1024
        ),
    )(psi, left_env, right_env.reshape(2 * BLOCK, BLOCK), sector_lengths, op_map.T)


def solution(mesh):
    in_specs = (P("op", "right"), P("op", "right", None), P("op", "right", None), P(), P())
    return jax.shard_map(
        on_device, mesh=mesh, in_specs=in_specs, out_specs=P("op", "right"), check_vma=False
    )
```
